1024 devices in a mesh: node: 64 (over x, z), local: 16 (over y, core).
Axes of the slice: x: 4, y: 8, z: 16, core: 2. Of those that a mesh axis runs over, the one named last changes fastest.
Arguments:
- tokens: bfloat16 [4096, 3584], P(('node', 'local')), may hold values from -6 to 6
- expert_ids: int32 [4096, 6], P(('node', 'local')), may hold values from 0 to 127, as said below
- gate_codes: int32 [4096, 6], P(('node', 'local')), may hold values from 1 to 1023
- gate_proj: bfloat16 [3584, 131072], P(None, ('node', 'local')), may hold values from -0.09375 to 0.09375
- up_proj: bfloat16 [3584, 131072], P(None, ('node', 'local')), may hold values from -0.09375 to 0.09375
- down_proj: bfloat16 [131072, 3584], P('node', 'local'), may hold values from -0.1875 to 0.1875
Outputs:
- routed: bfloat16 [4096, 3584], P(('node', 'local'))
The draws below stay inside these ranges and needn't reach their ends.
Inputs may be any that keep to these rules, and one draw needn't show every extreme that they name: `expert_ids`: each token names 6 different experts, lying in exactly 4 node groups with at least one named expert in each. The tokens of one device name each node group at most 1 times in all and some node group exactly 1 times; where 64 divides 4 * 4, they name every node group exactly 1 times. For every local index, the tokens of all devices with that local index together name each node group exactly 4 * 4 times.
All inputs are finite; a program needn't handle non-finite values.
Results may differ from the reference program's by a relative error of at most 0.02.
Values may be sent and summed in bfloat16 or wider, within the bound.
A program may use at most 32 MiB of HBM per device.

```python
import jax
import jax.numpy as jnp
from jax import lax

D = 3584
FF_E = 1024
EXP_NODE = 2
NL = 4
TOP = 6
TOK_DEV = 4
EXPERTS = 128
TOKENS = 4096
N_NODE = 64
N_LOCAL = 16


def draw_expert_ids(key, part):
    key_offset, key_mapping, key_drop = jax.random.split(key, 3)
    offsets = jax.vmap(lambda single: jax.random.permutation(single, N_NODE))(jax.random.split(key_offset, N_LOCAL))
    mapping = jax.vmap(lambda single: jax.random.permutation(single, N_NODE))(jax.random.split(key_mapping, N_LOCAL))
    node_index = jnp.arange(N_NODE, dtype=jnp.int32)[:, None, None, None]
    lane_index = jnp.arange(N_LOCAL, dtype=jnp.int32)[None, :, None, None]
    choice_index = jnp.arange(TOK_DEV, dtype=jnp.int32)[None, None, :, None] * NL + jnp.arange(NL, dtype=jnp.int32)[None, None, None, :]
    shifted = offsets[lane_index, choice_index % N_NODE]
    target = mapping[lane_index, (node_index + shifted) % N_NODE]
    shape = (N_NODE, N_LOCAL, TOK_DEV)
    key_first, key_second, key_side = jax.random.split(key_drop, 3)
    first = jax.random.randint(key_first, shape, 0, NL)
    second = (first + jax.random.randint(key_second, shape, 1, NL)) % NL
    sides = jax.random.randint(key_side, shape + (2,), 0, EXP_NODE)
    candidates = target[..., None] * EXP_NODE + jnp.arange(EXP_NODE, dtype=jnp.int32)
    slot_k = jnp.arange(NL, dtype=jnp.int32)[:, None]
    slot_e = jnp.arange(EXP_NODE, dtype=jnp.int32)[None, :]
    dropped = (slot_k == first[..., None, None]) & (slot_e == sides[..., 0, None, None]) | (slot_k == second[..., None, None]) & (slot_e == sides[..., 1, None, None])
    flat_cand = candidates.reshape(shape + (NL * EXP_NODE,))
    flat_drop = dropped.reshape(shape + (NL * EXP_NODE,)).astype(jnp.int32)
    keyed = flat_drop * (NL * EXP_NODE) + jnp.arange(NL * EXP_NODE, dtype=jnp.int32)
    kept = jnp.argsort(keyed, axis=-1)[..., :TOP]
    picked = jnp.take_along_axis(flat_cand, kept, axis=-1)
    return picked.reshape(N_NODE * N_LOCAL * TOK_DEV, TOP).astype(jnp.int32)


def touch_ends(result, own_key, least, largest):
    extent = result.shape
    spot = [jax.random.randint(jax.random.fold_in(own_key, axis), (), 0, extent[axis]) for axis in range(len(extent))]
    result = result.at[tuple(spot)].set(least)
    longest = extent.index(max(extent))
    spot[longest] = (spot[longest] + 1) % extent[longest]
    return result.at[tuple(spot)].set(largest)


def steps_of(stream_key, shape, shards, low, largest):
    loudness = 1.0
    for axis_at, blocks in shards:
        draws = jax.random.uniform(jax.random.fold_in(jax.random.fold_in(stream_key, 6), axis_at), (blocks,), jnp.float32, low / len(shards), largest / len(shards))
        loudness = loudness * jnp.repeat(jnp.exp(draws), shape[axis_at] // blocks).reshape((-1,) + (1,) * (len(shape) - 1 - axis_at))
    return loudness


def normal_values(rng, shape, deviation, reach, pieces=(), kind=jnp.bfloat16):
    level = steps_of(rng, shape, pieces, -0.22, 0.18) if pieces else 1.0
    array = jax.random.normal(rng, shape, jnp.float32) * deviation * level
    return jnp.minimum(jnp.maximum(array, -reach), reach).astype(kind)


def setup_inputs(seed: int = 0) -> dict:
    splits = jax.random.split(jax.random.key(seed), 7)
    return {
        "tokens": normal_values(splits[0], (TOKENS, D), 1.0, 6.0, ((0, 1024),)),
        "expert_ids": draw_expert_ids(jax.random.fold_in(splits[6], 71), 0),
        "gate_codes": touch_ends(jax.random.randint(splits[2], (TOKENS, TOP), 1, 1024), jax.random.fold_in(splits[2], 1), 1, 1023).astype(jnp.int32),
        "gate_proj": normal_values(splits[3], (D, EXPERTS * FF_E), D ** -0.5, 0.09375, ((1, 1024),)),
        "up_proj": normal_values(splits[4], (D, EXPERTS * FF_E), D ** -0.5, 0.09375, ((1, 1024),)),
        "down_proj": normal_values(splits[5], (EXPERTS * FF_E, D), FF_E ** -0.5, 0.1875, ((0, 64), (1, 16))),
    }


ROUTE_SCALE = 2.5


def reference(tokens, expert_ids, gate_codes, gate_proj, up_proj, down_proj):
    codes_float = gate_codes.astype(jnp.float32)
    weights = ROUTE_SCALE * codes_float / jnp.sum(codes_float, axis=1, keepdims=True)
    node_of = expert_ids // EXP_NODE
    expert_side = expert_ids % EXP_NODE
    node_rows = N_LOCAL * TOK_DEV * NL
    node_width = EXP_NODE * FF_E

    def one_group(summed, node_group):
        node_hit = node_of == node_group
        node_used = jnp.any(node_hit, axis=1).astype(jnp.int32)
        picked = jnp.argsort(1 - node_used, stable=True)[:node_rows].astype(jnp.int32)
        chosen = jnp.take(tokens, picked, axis=0)
        gate_pair = jnp.stack(
            [jnp.sum(jnp.where(node_hit & (expert_side == side_index), weights, 0.0), axis=1)
             for side_index in range(EXP_NODE)], axis=1)
        gate_pair = jnp.take(gate_pair, picked, axis=0)
        start_col = (node_group * node_width).astype(jnp.int32)
        gate_block = lax.dynamic_slice_in_dim(gate_proj, start_col, node_width, 1)
        up_block = lax.dynamic_slice_in_dim(up_proj, start_col, node_width, 1)
        down_block = lax.dynamic_slice_in_dim(down_proj, start_col, node_width, 0)
        pre_gate = jnp.dot(chosen, gate_block, preferred_element_type=jnp.float32)
        pre_up = jnp.dot(chosen, up_block, preferred_element_type=jnp.float32)
        gate_scale = jnp.repeat(gate_pair, FF_E, axis=1)
        hidden = (gate_scale * jax.nn.silu(pre_gate) * pre_up).astype(jnp.bfloat16)
        contrib = jnp.dot(hidden, down_block, preferred_element_type=jnp.float32).astype(jnp.bfloat16)
        summed = summed.at[picked].add(contrib.astype(jnp.float32))
        return summed, None

    summed, ignored = lax.scan(one_group, jnp.zeros(tokens.shape, jnp.float32),
                               jnp.arange(N_NODE, dtype=jnp.int32))
    return summed.astype(jnp.bfloat16)
```

```python
import functools

import jax
import jax.numpy as jnp
from jax import lax
from jax.experimental import pallas as pl
from jax.experimental.pallas import tpu as pltpu
from jax.sharding import PartitionSpec as P

NX, NZ, NY = 4, 16, 8
TOK = 4
SEG = 4
ROWS = 16
FF_E = 1024
ROUTE_SCALE = 2.5
SENDS = 64
MESH = pl.DeviceIdType.MESH
F32, BF16, I32 = jnp.float32, jnp.bfloat16, jnp.int32


def log2(n):
    return n.bit_length() - 1


def dot(a, b):
    return jnp.dot(a, b, preferred_element_type=F32)


def dot_nt(a, b):
    return lax.dot_general(a, b, (((1,), (1,)), ((), ())), preferred_element_type=F32)


def iota(shape, axis):
    return lax.broadcasted_iota(I32, shape, axis)


def hot(mask):
    return jnp.where(mask, 1.0, 0.0).astype(BF16)


def arrival_order():
    order = [0]
    for k in range(1, NZ // 2):
        order += [k, NZ - k]
    return order + [NZ // 2]


class Sender:
    def __init__(self, sems):
        self.sems, self.live, self.count = sems, {}, 0

    def __call__(self, src, dst, recv_sem, device):
        slot = self.count % SENDS
        if slot in self.live:
            self.live[slot].wait_send()
        copy = pltpu.make_async_remote_copy(
            src_ref=src, dst_ref=dst, send_sem=self.sems.at[slot], recv_sem=recv_sem,
            device_id=device, device_id_type=MESH,
        )
        copy.start()
        self.live[slot] = copy
        self.count += 1

    def arrived(self, dst, recv_sem, device):
        pltpu.make_async_remote_copy(
            src_ref=dst, dst_ref=dst, send_sem=self.sems.at[0], recv_sem=recv_sem,
            device_id=device, device_id_type=MESH,
        ).wait_recv()

    def drain(self):
        for copy in self.live.values():
            copy.wait_send()


def kernel(tok_ref, ids_ref, codes_ref, gate_hbm, up_hbm, down_hbm, out_ref,
           w_in, w_down, zb, xs, xr, xg, xm, hg, acc, ex, rs, rr, sb, rb, fs, fr,
           wsem, ssem, zsem, xsem, ysem, ymsem, psem, pmsem, hsem, hpsem, rsem, bsem, fsem):
    lanes_n = 2 * NY
    width = tok_ref.shape[1]
    seg_len = width // SEG
    feats = down_hbm.shape[0]
    half = NY // 2

    node, loc = lax.axis_index("node"), lax.axis_index("local")
    x, z = lax.div(node, NZ), lax.rem(node, NZ)
    y, core = lax.div(loc, 2), lax.rem(loc, 2)
    z_right = (x * NZ + lax.rem(z + 1, NZ), loc)
    z_left = (x * NZ + lax.rem(z + NZ - 1, NZ), loc)

    def x_dev(d):
        return (lax.rem(x + d, NX) * NZ + z, loc)

    def chip(d):
        return lax.rem(y + d + NY, NY)

    y_devs = ((node, chip(1) * 2 + core), (node, chip(-1) * 2 + core))
    partner = (node, y * 2 + 1 - core)

    barrier = pltpu.get_barrier_semaphore()
    friends = [z_right, z_left] + [x_dev(d) for d in range(1, NX)]
    friends += [(node, lax.rem(loc + k, lanes_n)) for k in range(1, lanes_n)]
    for friend in friends:
        pl.semaphore_signal(barrier, inc=1, device_id=friend, device_id_type=MESH)

    weight_copies = [
        pltpu.make_async_copy(gate_hbm, w_in.at[:, pl.ds(0, 128)], wsem.at[0]),
        pltpu.make_async_copy(up_hbm, w_in.at[:, pl.ds(128, 128)], wsem.at[1]),
        pltpu.make_async_copy(down_hbm, w_down.at[pl.ds(0, feats)], wsem.at[2]),
    ]
    for copy in weight_copies:
        copy.start()
    if feats < 256:
        w_down[pl.ds(feats, 256 - feats), :] = jnp.zeros((256 - feats, w_down.shape[1]), BF16)

    tokens = tok_ref[...].astype(F32)
    lane4 = iota((TOK, 128), 1)
    ids, codes = ids_ref[...], codes_ref[...].astype(F32)
    total = jnp.sum(codes, axis=1, keepdims=True)
    dense = jnp.zeros((TOK, 128), F32)
    for p in range(ids.shape[1]):
        dense += jnp.where(lane4 == ids[:, p : p + 1], codes[:, p : p + 1], 0.0)
    dense = ROUTE_SCALE * dense / total
    zb[0, :, pl.ds(0, seg_len)] = jnp.concatenate(
        [tokens[:, s * seg_len : (s + 1) * seg_len] for s in range(SEG)], axis=0
    ).astype(BF16)
    zb[0, :, pl.ds(seg_len, 128)] = jnp.concatenate([dense] * SEG, axis=0).astype(BF16)

    pl.semaphore_wait(barrier, len(friends))
    send = Sender(ssem)

    order = arrival_order()
    at = {j: p for p, j in enumerate(order)}
    sel_rows = NX * 16
    row = iota((sel_rows, 64), 0)
    col = iota((sel_rows, 64), 1)
    same_seg_block = (((row >> 2) & 3) == ((col >> 2) & 3)) & ((row & 3) == (col >> 4))
    row_e = iota((sel_rows, 128), 0)
    lane_e = iota((sel_rows, 128), 1)
    goal = ((x + (row_e >> 4)) & (NX - 1)) * NZ + z
    goal_hot = hot((lane_e >> 1) == goal)
    token_lane = lane_e == ((2 * goal + 2) & 127)
    token_value = ((iota((64, 128), 0) & 3) + 1).astype(F32).astype(BF16)

    def select(q):
        block = zb[pl.ds(4 * q, 4)].reshape(64, seg_len + 128)
        body, meta = block[:, :seg_len], block[:, seg_len:]
        picks = hot((dot_nt(goal_hot, meta) > 0.0) & same_seg_block)
        rows = dot(picks, body).astype(BF16)
        info = jnp.where(token_lane, dot(picks, token_value), dot(picks, meta)).astype(BF16)
        for d in list(range(1, NX)) + [0]:
            target = xs if d else xr
            target[d, q, :, pl.ds(0, seg_len)] = rows[d * 16 : (d + 1) * 16]
            target[d, q, :, pl.ds(seg_len, 128)] = info[d * 16 : (d + 1) * 16]
            if d:
                send(xs.at[d, q], xr.at[d, q], xsem.at[d, q], x_dev(d))

    def z_hop(j, j_there, device):
        send(zb.at[at[j]], zb.at[at[j_there]], zsem.at[at[j_there]], device)

    z_hop(0, 1, z_right)
    z_hop(0, NZ - 1, z_left)
    here, done = {0}, 0
    for k in range(1, NZ // 2 + 1):
        send.arrived(zb.at[at[k]], zsem.at[at[k]], z_left)
        here.add(at[k])
        if k < NZ // 2:
            z_hop(k, k + 1, z_right)
        if k < NZ // 2:
            j = NZ - k
            send.arrived(zb.at[at[j]], zsem.at[at[j]], z_right)
            here.add(at[j])
            if j - 1 > NZ // 2:
                z_hop(j, j - 1, z_left)
        while done < NZ // 4 and all(p in here for p in range(4 * done, 4 * done + 4)):
            select(done)
            done += 1

    for q in range(NZ // 4):
        for d in range(1, NX):
            send.arrived(xr.at[d, q], xsem.at[d, q], x_dev(NX - d))

    slots = NX * NZ * SEG
    gate_lane = 2 * node
    token_at = (2 * node + 2) & 127
    source_at = (2 * node + 3) & 127
    every = xr[...].reshape(slots, seg_len + 128)
    meta = every[:, seg_len:]
    live = dot_nt(hot(iota((SEG * ROWS, 128), 1) == token_at), meta) > 0.0
    ahead_r, ahead_c = iota((slots, slots), 0), iota((slots, slots), 1)

    def slot_of(r):
        return (r >> 4) * 4 + (r & 3)

    ahead = hot((((ahead_r >> 2) & 3) == ((ahead_c >> 2) & 3)) & (slot_of(ahead_r) < slot_of(ahead_c)))
    place = dot(hot(live), ahead)
    want_r, want_c = iota((SEG * ROWS, slots), 0), iota((SEG * ROWS, slots), 1)
    picks = hot(
        live & (place == (want_r & (ROWS - 1)).astype(F32)) & ((want_r >> 4) == ((want_c >> 2) & 3))
    )
    xg[loc] = dot(picks, every[:, :seg_len]).astype(BF16).reshape(SEG, ROWS, seg_len)
    slot_value = slot_of(iota((slots, 128), 0)).astype(F32).astype(BF16)
    first = picks[:ROWS]
    xm[loc] = jnp.where(
        iota((ROWS, 128), 1) == source_at, dot(first, slot_value), dot(first, meta)
    ).astype(BF16)

    def chip_lane(d, other=False):
        return chip(d) * 2 + (1 - core if other else core)

    def y_part(lane, h):
        return xg.at[lane, pl.ds(2 * h, 2)]

    def y_hop(way, k, lane, h):
        send(y_part(lane, h), y_part(lane, h), ysem.at[way, k, h], y_devs[way])
        if h == way and not (k == half and way):
            send(xm.at[lane], xm.at[lane], ymsem.at[way, k], y_devs[way])

    def y_wait(way, k, lane, h):
        send.arrived(y_part(lane, h), ysem.at[way, k, h], y_devs[1 - way])
        if h == way and not (k == half and way):
            send.arrived(xm.at[lane], ymsem.at[way, k], y_devs[1 - way])

    def p_hop(d, lane, h, with_meta):
        send(y_part(lane, h), y_part(lane, h), psem.at[d % NY, h], partner)
        if with_meta:
            send(xm.at[lane], xm.at[lane], pmsem.at[d % NY], partner)

    def p_wait(d):
        lane = chip_lane(d, True)
        for h in range(2):
            send.arrived(y_part(lane, h), psem.at[d % NY, h], partner)
        send.arrived(xm.at[lane], pmsem.at[d % NY], partner)

    def passes(k, way, h):
        return k < half or (k == half and h == way)

    my_expert = lax.div(loc * 128, FF_E)

    def gate_up(chips):
        lanes = []
        for d in chips:
            p_wait(d)
            lanes += [chip_lane(d), chip_lane(d, True)]
        lhs = jnp.concatenate(
            [jnp.concatenate([xg[lane, s] for lane in lanes], axis=0) for s in range(SEG)], axis=1
        )
        pre = dot(lhs, w_in[...])
        info = jnp.concatenate([xm[lane] for lane in lanes], axis=0).astype(F32)
        gate = jnp.sum(
            jnp.where(iota(info.shape, 1) == gate_lane + my_expert, info, 0.0), axis=1, keepdims=True
        )
        g, u = pre[:, :128], pre[:, 128:]
        hidden = (gate * (g / (1.0 + jnp.exp(-g))) * u).astype(BF16)
        for n, lane in enumerate(lanes):
            hg[loc, lane] = hidden[n * ROWS : (n + 1) * ROWS]

    for h in range(2):
        for way in range(2):
            if passes(1, way, h):
                y_hop(way, 1, loc, h)
        p_hop(0, loc, h, h == 0)
    for copy in weight_copies:
        copy.wait()
    for k in range(1, half + 1):
        for h in range(2):
            for way in range(2):
                if passes(k, way, h):
                    d = -k if way == 0 else k
                    lane = chip_lane(d)
                    y_wait(way, k, lane, h)
                    if passes(k + 1, way, h):
                        y_hop(way, k + 1, lane, h)
                    p_hop(d, lane, h, h == way if k < half else way == 0)
        gate_up([0] if k == 1 else [-(k - 1), k - 1])
    gate_up([half])

    def h_part(lane, h):
        return hg.at[lane, pl.ds(h * NY, NY)]

    def h_hop(way, k, lane, h):
        send(h_part(lane, h), h_part(lane, h), hsem.at[way, k, h], y_devs[way])

    def hp_hop(d, lane, h):
        send(h_part(lane, h), h_part(lane, h), hpsem.at[d % NY, h], partner)

    for h in range(2):
        for way in range(2):
            if passes(1, way, h):
                h_hop(way, 1, loc, h)
        hp_hop(0, loc, h)

    group_rows = lanes_n * ROWS
    back_rows = NZ * lanes_n
    info = xm[...].reshape(group_rows, 128)
    source = dot_nt(hot(iota((back_rows, 128), 1) == source_at), info)
    back_r, back_c = iota((back_rows, group_rows), 0), iota((back_rows, group_rows), 1)
    lane_match = (back_r & (lanes_n - 1)) == (back_c >> 4)
    back_slot = NZ - 1 - (back_r >> log2(lanes_n))
    for d in range(NX):
        ex[d] = hot(lane_match & (source == (back_slot + d * NZ).astype(F32)))
    token_col = jnp.sum(
        jnp.where(iota((group_rows, 128), 1) == token_at, info.astype(F32), 0.0), axis=1, keepdims=True
    )

    acc[...] = jnp.zeros(acc.shape, F32)

    def down(chips):
        for d in chips:
            for h in range(2):
                send.arrived(h_part(chip_lane(d, True), h), hpsem.at[d % NY, h], partner)
            lhs = jnp.concatenate(
                [hg[chip(d) * 2 + c].reshape(group_rows, 128) for c in range(2)], axis=1
            )
            at_col = pl.multiple_of(chip(d) * 256, 256)
            acc[...] += dot_nt(lhs, w_down[:, pl.ds(at_col, 256)])

    for k in range(1, half + 1):
        for h in range(2):
            for way in range(2):
                if passes(k, way, h):
                    d = -k if way == 0 else k
                    lane = chip_lane(d)
                    send.arrived(h_part(lane, h), hsem.at[way, k, h], y_devs[1 - way])
                    if passes(k + 1, way, h):
                        h_hop(way, k + 1, lane, h)
                    hp_hop(d, lane, h)
        down([0] if k == 1 else [-(k - 1), k - 1])
    down([half])

    result = jnp.where(iota((group_rows, 256), 1) == feats, token_col, acc[...]).astype(BF16)
    for q in range(NZ // 4):
        for d in list(range(1, NX)) + [0]:
            rows = dot(ex[d, pl.ds(q * 4 * lanes_n, 4 * lanes_n)], result).astype(BF16)
            target = rs if d else rr
            target[d, pl.ds(4 * q, 4)] = rows.reshape(4, lanes_n, 256)
            if d:
                send(rs.at[d, pl.ds(4 * q, 4)], rr.at[d, pl.ds(4 * q, 4)], rsem.at[d, q], x_dev(NX - d))

    seen = set()

    def part(j):
        p = NZ - 1 - at[j]
        q = p // 4
        if q not in seen:
            seen.add(q)
            for d in range(1, NX):
                send.arrived(rr.at[d, pl.ds(4 * q, 4)], rsem.at[d, q], x_dev(d))
        sums = [jnp.zeros((lanes_n, 256), F32) for t in range(TOK)]
        for d in range(NX):
            rows = rr[d, p].astype(F32)
            which = jnp.sum(
                jnp.where(iota((lanes_n, 256), 1) == feats, rows, 0.0), axis=1, keepdims=True
            )
            for t in range(TOK):
                sums[t] += jnp.where(which == float(t + 1), rows, 0.0)
        return jnp.concatenate(sums, axis=0)

    for s in range(NZ // 2):
        for j, step, device, source_dev in (
            (NZ // 2 - s, -1, z_left, z_right),
            (NZ // 2 + 1 + s, 1, z_right, z_left),
        ):
            if j >= NZ:
                continue
            value = part(j)
            if s:
                send.arrived(rb.at[j], bsem.at[j], source_dev)
                value += rb[j].astype(F32)
            sb[j] = value.astype(BF16)
            send(sb.at[j], rb.at[j + step], bsem.at[j + step], device)
    value = part(0)
    send.arrived(rb.at[NZ], bsem.at[NZ], z_left)
    value += rb[NZ].astype(F32)
    send.arrived(rb.at[0], bsem.at[0], z_right)
    value = (value + rb[0].astype(F32)).astype(BF16)

    fin_r, fin_c = iota((lanes_n * 8, TOK * lanes_n), 0), iota((lanes_n * 8, TOK * lanes_n), 1)
    fin = ((fin_r >> 3) == (fin_c & (lanes_n - 1))) & ((fin_r & 3) == (fin_c >> log2(lanes_n)))
    upper = ((fin_r >> 2) & 1) == 1
    rows = dot(hot(fin & jnp.logical_not(upper)), value[:, :128]) + dot(hot(fin & upper), value[:, 128:])
    fs[...] = rows.astype(BF16).reshape(lanes_n, 8, 128)
    for k in range(1, lanes_n):
        lane = lax.rem(loc + k, lanes_n)
        send(fs.at[lane], fr.at[loc], fsem.at[k], (node, lane))
    out_ref[loc] = fs[loc]
    for k in range(1, lanes_n):
        lane = lax.rem(loc + lanes_n - k, lanes_n)
        send.arrived(fr.at[lane], fsem.at[k], (node, lane))
        out_ref[lane] = fr[lane]
    send.drain()


def on_device(tokens, expert_ids, gate_codes, gate_proj, up_proj, down_proj):
    width = tokens.shape[1]
    seg_len = width // SEG
    lanes_n = 2 * NY
    hidden, feats = down_proj.shape
    dma = pltpu.SemaphoreType.DMA
    vmem = pl.BlockSpec(memory_space=pltpu.VMEM)
    hbm = pl.BlockSpec(memory_space=pltpu.HBM)
    half = NY // 2
    pieces = pl.pallas_call(
        kernel,
        out_shape=jax.ShapeDtypeStruct((lanes_n, 8, 128), BF16),
        in_specs=[vmem, vmem, vmem, hbm, hbm, hbm],
        out_specs=vmem,
        scratch_shapes=[
            pltpu.VMEM((width, 256), BF16),
            pltpu.VMEM((256, hidden), BF16),
            pltpu.VMEM((NZ, 16, seg_len + 128), BF16),
            pltpu.VMEM((NX, NZ // 4, 16, seg_len + 128), BF16),
            pltpu.VMEM((NX, NZ // 4, 16, seg_len + 128), BF16),
            pltpu.VMEM((lanes_n, SEG, ROWS, seg_len), BF16),
            pltpu.VMEM((lanes_n, ROWS, 128), BF16),
            pltpu.VMEM((lanes_n, lanes_n, ROWS, 128), BF16),
            pltpu.VMEM((lanes_n * ROWS, 256), F32),
            pltpu.VMEM((NX, NZ * lanes_n, lanes_n * ROWS), BF16),
            pltpu.VMEM((NX, NZ, lanes_n, 256), BF16),
            pltpu.VMEM((NX, NZ, lanes_n, 256), BF16),
            pltpu.VMEM((NZ, TOK * lanes_n, 256), BF16),
            pltpu.VMEM((NZ + 1, TOK * lanes_n, 256), BF16),
            pltpu.VMEM((lanes_n, 8, 128), BF16),
            pltpu.VMEM((lanes_n, 8, 128), BF16),
            dma((3,)),
            dma((SENDS,)),
            dma((NZ,)),
            dma((NX, NZ // 4)),
            dma((2, half + 1, 2)),
            dma((2, half + 1)),
            dma((NY, 2)),
            dma((NY,)),
            dma((2, half + 1, 2)),
            dma((NY, 2)),
            dma((NX, NZ // 4)),
            dma((NZ + 1,)),
            dma((lanes_n,)),
        ],
        compiler_params=pltpu.CompilerParams(
            collective_id=0, has_side_effects=True, vmem_limit_bytes=48 << 20
        ),
        name="moe",
    )(tokens, expert_ids, gate_codes, gate_proj, up_proj, down_proj.T)
    pieces = pieces.reshape(lanes_n, 2, TOK, 128).transpose(2, 0, 1, 3).reshape(TOK, lanes_n, 256)
    return pieces[:, :, :feats].reshape(TOK, width)


def solution(mesh):
    return jax.shard_map(
        on_device,
        mesh=mesh,
        in_specs=(
            P(("node", "local"), None),
            P(("node", "local"), None),
            P(("node", "local"), None),
            P(None, ("node", "local")),
            P(None, ("node", "local")),
            P("node", "local"),
        ),
        out_specs=P(("node", "local"), None),
        check_vma=False,
    )
```

```python
import functools

import jax
import jax.numpy as jnp
from jax import lax
from jax.experimental import pallas as pl
from jax.experimental.pallas import tpu as pltpu
from jax.sharding import PartitionSpec as P

NX, NZ, NY = 4, 16, 8
TOK = 4
SEG = 4
ROWS = 16
FF_E = 1024
ROUTE_SCALE = 2.5
SENDS = 64
STRIDE = 2
PARTS = 2
MESH = pl.DeviceIdType.MESH
F32, BF16, I32 = jnp.float32, jnp.bfloat16, jnp.int32


def log2(n):
    return n.bit_length() - 1


def dot(a, b):
    return jnp.dot(a, b, preferred_element_type=F32)


def dot_nt(a, b):
    return lax.dot_general(a, b, (((1,), (1,)), ((), ())), preferred_element_type=F32)


def iota(shape, axis):
    return lax.broadcasted_iota(I32, shape, axis)


def hot(mask):
    return jnp.where(mask, 1.0, 0.0).astype(BF16)


def arrival_order():
    order = [0]
    for k in range(1, NZ // 2):
        order += [k, NZ - k]
    return order + [NZ // 2]


class Sender:
    def __init__(self, sems):
        self.sems, self.live, self.count = sems, {}, 0

    def __call__(self, src, dst, recv_sem, device):
        slot = self.count % SENDS
        if slot in self.live:
            self.live[slot].wait_send()
        copy = pltpu.make_async_remote_copy(
            src_ref=src, dst_ref=dst, send_sem=self.sems.at[slot], recv_sem=recv_sem,
            device_id=device, device_id_type=MESH,
        )
        copy.start()
        self.live[slot] = copy
        self.count += 1

    def arrived(self, dst, recv_sem, device):
        pltpu.make_async_remote_copy(
            src_ref=dst, dst_ref=dst, send_sem=self.sems.at[0], recv_sem=recv_sem,
            device_id=device, device_id_type=MESH,
        ).wait_recv()

    def drain(self):
        for copy in self.live.values():
            copy.wait_send()


def kernel(tok_hbm, ids_hbm, codes_hbm, gate_hbm, up_hbm, down_hbm, out_ref,
           tok_ref, ids_ref, codes_ref, w_in, w_down, zb, xs, xr, xg, xm, hg, acc, token_col, ex, rs, rr, sb, rb, fs, fr,
           wsem, ssem, zsem, xsem, ysem, ymsem, psem, pmsem, hsem, hpsem, rsem, bsem, fsem):
    lanes_n = 2 * NY
    width = tok_hbm.shape[1]
    seg_len = width // SEG
    feats = down_hbm.shape[0]
    half = NY // 2

    node, loc = lax.axis_index("node"), lax.axis_index("local")
    x, z = lax.div(node, NZ), lax.rem(node, NZ)
    y, core = lax.div(loc, 2), lax.rem(loc, 2)

    def z_dev(d):
        return (x * NZ + lax.rem(z + d + NZ, NZ), loc)

    def x_dev(d):
        return (lax.rem(x + d, NX) * NZ + z, loc)

    def chip(d):
        return lax.rem(y + d + NY, NY)

    y_devs = ((node, chip(1) * 2 + core), (node, chip(-1) * 2 + core))
    partner = (node, y * 2 + 1 - core)

    input_copies = [
        pltpu.make_async_copy(tok_hbm, tok_ref, wsem.at[3]),
        pltpu.make_async_copy(ids_hbm, ids_ref, wsem.at[4]),
        pltpu.make_async_copy(codes_hbm, codes_ref, wsem.at[5]),
    ]
    for copy in input_copies:
        copy.start()
    barrier = pltpu.get_barrier_semaphore()
    friends = [z_dev(way * d) for d in range(1, STRIDE + 1) for way in (1, -1)]
    friends += [x_dev(d) for d in range(1, NX)]
    friends += [(node, lax.rem(loc + k, lanes_n)) for k in range(1, lanes_n)]
    for friend in friends:
        pl.semaphore_signal(barrier, inc=1, device_id=friend, device_id_type=MESH)

    weight_copies = [
        pltpu.make_async_copy(gate_hbm, w_in.at[:, pl.ds(0, 128)], wsem.at[0]),
        pltpu.make_async_copy(up_hbm, w_in.at[:, pl.ds(128, 128)], wsem.at[1]),
        pltpu.make_async_copy(down_hbm, w_down.at[pl.ds(0, feats)], wsem.at[2]),
    ]
    for copy in weight_copies:
        copy.start()
    if feats < 256:
        w_down[pl.ds(feats, 256 - feats), :] = jnp.zeros((256 - feats, w_down.shape[1]), BF16)

    for copy in input_copies:
        copy.wait()
    tokens = tok_ref[...].astype(F32)
    lane4 = iota((TOK, 128), 1)
    ids, codes = ids_ref[...], codes_ref[...].astype(F32)
    total = jnp.sum(codes, axis=1, keepdims=True)
    dense = jnp.zeros((TOK, 128), F32)
    for p in range(ids.shape[1]):
        dense += jnp.where(lane4 == ids[:, p : p + 1], codes[:, p : p + 1], 0.0)
    dense = ROUTE_SCALE * dense / total
    body = jnp.concatenate([tokens[:, s * seg_len : (s + 1) * seg_len] for s in range(SEG)], axis=0)
    block = jnp.concatenate([body, jnp.concatenate([dense] * SEG, axis=0)], axis=1).astype(BF16)
    cut = (seg_len + 128) // PARTS
    for c in range(PARTS):
        zb[0, c] = block[:, c * cut : (c + 1) * cut]

    pl.semaphore_wait(barrier, len(friends))
    send = Sender(ssem)

    order = arrival_order()
    at = {j: p for p, j in enumerate(order)}
    sel_rows = NX * 16
    row = iota((sel_rows, 64), 0)
    col = iota((sel_rows, 64), 1)
    same_seg_block = (((row >> 2) & 3) == ((col >> 2) & 3)) & ((row & 3) == (col >> 4))
    row_e = iota((sel_rows, 128), 0)
    lane_e = iota((sel_rows, 128), 1)
    goal = ((x + (row_e >> 4)) & (NX - 1)) * NZ + z
    goal_hot = hot((lane_e >> 1) == goal)
    token_lane = lane_e == ((2 * goal + 2) & 127)
    token_value = ((iota((64, 128), 0) & 3) + 1).astype(F32).astype(BF16)

    x_order = [NX // 2] + [d for d in range(1, NX) if d != NX // 2] + [0]

    def select(q):
        block = jnp.concatenate([zb[pl.ds(4 * q, 4), c].reshape(64, cut) for c in range(PARTS)], axis=1)
        body, meta = block[:, :seg_len], block[:, seg_len:]
        picks = hot((dot_nt(goal_hot, meta) > 0.0) & same_seg_block)
        rows = dot(picks, body).astype(BF16)
        info = jnp.where(token_lane, dot(picks, token_value), dot(picks, meta)).astype(BF16)
        for d in x_order:
            target = xs if d else xr
            target[d, q, :, pl.ds(0, seg_len)] = rows[d * 16 : (d + 1) * 16]
            target[d, q, :, pl.ds(seg_len, 128)] = info[d * 16 : (d + 1) * 16]
            if d:
                send(xs.at[d, q], xr.at[d, q], xsem.at[d, q], x_dev(d))

    reach = {1: NZ // 2, -1: NZ // 2 - 1}

    def z_hop(way, k, step, c):
        here, there = at[way * k % NZ], at[way * (k + step) % NZ]
        send(zb.at[here, c], zb.at[there, c], zsem.at[there, c], z_dev(way * step))

    def z_relay(way, k, c):
        for step in [STRIDE] + list(range(1, STRIDE)):
            if k % STRIDE == 0 and k + step <= reach[way]:
                z_hop(way, k, step, c)

    for c in range(PARTS):
        for way in (1, -1):
            z_relay(way, 0, c)
    here, done = {0}, 0
    for base in range(0, NZ // 2, STRIDE):
        for k in [base + STRIDE] + list(range(base + 1, base + STRIDE)):
            for c in range(PARTS):
                for way in (1, -1):
                    if k <= reach[way]:
                        p = at[way * k % NZ]
                        back = STRIDE if k % STRIDE == 0 else k % STRIDE
                        send.arrived(zb.at[p, c], zsem.at[p, c], z_dev(-way * back))
                        z_relay(way, k, c)
                        here.add(p)
        while done < NZ // 4 and all(p in here for p in range(4 * done, 4 * done + 4)):
            select(done)
            done += 1

    for q in range(NZ // 4):
        for d in range(1, NX):
            send.arrived(xr.at[d, q], xsem.at[d, q], x_dev(NX - d))

    slots = NX * NZ * SEG
    gate_lane = 2 * node
    token_at = (2 * node + 2) & 127
    source_at = (2 * node + 3) & 127
    every = xr[...].reshape(slots, seg_len + 128)
    meta = every[:, seg_len:]
    live = dot_nt(hot(iota((SEG * ROWS, 128), 1) == token_at), meta) > 0.0
    ahead_r, ahead_c = iota((slots, slots), 0), iota((slots, slots), 1)

    def slot_of(r):
        return (r >> 4) * 4 + (r & 3)

    ahead = hot((((ahead_r >> 2) & 3) == ((ahead_c >> 2) & 3)) & (slot_of(ahead_r) < slot_of(ahead_c)))
    place = dot(hot(live), ahead)
    want_r, want_c = iota((SEG * ROWS, slots), 0), iota((SEG * ROWS, slots), 1)
    picks = hot(
        live & (place == (want_r & (ROWS - 1)).astype(F32)) & ((want_r >> 4) == ((want_c >> 2) & 3))
    )
    xg[loc] = dot(picks, every[:, :seg_len]).astype(BF16).reshape(SEG, ROWS, seg_len)
    slot_value = slot_of(iota((slots, 128), 0)).astype(F32).astype(BF16)
    first = picks[:ROWS]
    xm[loc] = jnp.where(
        iota((ROWS, 128), 1) == source_at, dot(first, slot_value), dot(first, meta)
    ).astype(BF16)

    def chip_lane(d, other=False):
        return chip(d) * 2 + (1 - core if other else core)

    def y_part(lane, h):
        return xg.at[lane, pl.ds(2 * h, 2)]

    def y_hop(way, k, lane, h):
        send(y_part(lane, h), y_part(lane, h), ysem.at[way, k, h], y_devs[way])
        if h == way and not (k == half and way):
            send(xm.at[lane], xm.at[lane], ymsem.at[way, k], y_devs[way])

    def y_wait(way, k, lane, h):
        send.arrived(y_part(lane, h), ysem.at[way, k, h], y_devs[1 - way])
        if h == way and not (k == half and way):
            send.arrived(xm.at[lane], ymsem.at[way, k], y_devs[1 - way])

    def p_hop(d, lane, h, with_meta):
        send(y_part(lane, h), y_part(lane, h), psem.at[d % NY, h], partner)
        if with_meta:
            send(xm.at[lane], xm.at[lane], pmsem.at[d % NY], partner)

    def p_wait(d):
        lane = chip_lane(d, True)
        for h in range(2):
            send.arrived(y_part(lane, h), psem.at[d % NY, h], partner)
        send.arrived(xm.at[lane], pmsem.at[d % NY], partner)

    def passes(k, way, h):
        return k < half or (k == half and h == way)

    my_expert = lax.div(loc * 128, FF_E)

    pieces = [[0] + ([-1, 1] if half > 1 else [])] + [[-k, k] for k in range(2, half)] + [[half]]
    starts = [sum(len(p) for p in pieces[:i]) for i in range(len(pieces))]
    slot = {d % NY: n for n, d in enumerate(d for p in pieces for d in p)}
    strides = [1 if i < len(pieces) - 2 else 2 for i in range(len(pieces))]

    def h_part(i, lane, k=0, way=0):
        n = 2 * len(pieces[i])
        if k < half:
            return hg.at[lane, pl.ds(2 * starts[i], n)]
        return hg.at[lane, pl.ds(2 * starts[i] + way * (n // 2), n // 2)]

    def y_dev(d):
        return (node, chip_lane(d))

    def h_relay(i, way, k, lane):
        for step in range(strides[i], 0, -1):
            if k % strides[i] == 0 and k + step <= half:
                part = h_part(i, lane, k + step, way)
                send(part, part, hsem.at[i, way, k + step], y_dev(step if way == 0 else -step))

    def hp_hop(i, lane, d, k=0, way=0):
        sem = hpsem.at[i, NY if k == half and way else d % NY]
        send(h_part(i, lane, k, way), h_part(i, lane, k, way), sem, partner)

    def gate_up(i):
        lanes = []
        for d in pieces[i]:
            p_wait(d)
            lanes += [chip(d) * 2, chip(d) * 2 + 1]
        lhs = jnp.concatenate(
            [jnp.concatenate([xg[lane, s] for lane in lanes], axis=0) for s in range(SEG)], axis=1
        )
        pre = dot(lhs, w_in[...])
        info = jnp.concatenate([xm[lane] for lane in lanes], axis=0).astype(F32)
        gate = jnp.sum(
            jnp.where(iota(info.shape, 1) == gate_lane + my_expert, info, 0.0), axis=1, keepdims=True
        )
        g, u = pre[:, :128], pre[:, 128:]
        hidden = (gate * (g / (1.0 + jnp.exp(-g))) * u).astype(BF16)
        for n in range(len(lanes)):
            hg[loc, 2 * starts[i] + n] = hidden[n * ROWS : (n + 1) * ROWS]
        hp_hop(i, loc, 0)
        for way in range(2):
            h_relay(i, way, 0, loc)

    def h_step(i, k):
        for way in range(2):
            d = -k if way == 0 else k
            lane = chip_lane(d)
            back = k % strides[i] or strides[i]
            send.arrived(h_part(i, lane, k, way), hsem.at[i, way, k], y_dev(-back if way == 0 else back))
            h_relay(i, way, k, lane)
            hp_hop(i, lane, d, k, way)

    def token_step(k):
        for h in range(2):
            for way in range(2):
                if passes(k, way, h):
                    d = -k if way == 0 else k
                    lane = chip_lane(d)
                    y_wait(way, k, lane, h)
                    p_hop(d, lane, h, h == way if k < half else way == 0)
                    if passes(k + 1, way, h):
                        y_hop(way, k + 1, lane, h)

    group_rows = lanes_n * ROWS
    back_rows = NZ * lanes_n

    def return_map():
        info = jnp.concatenate([xm[chip(d) * 2 + c] for d in range(NY) for c in range(2)], axis=0)
        source = dot_nt(hot(iota((back_rows, 128), 1) == source_at), info)
        back_r, back_c = iota((back_rows, group_rows), 0), iota((back_rows, group_rows), 1)
        from_lane = ((y + (back_c >> 5)) & (NY - 1)) * 2 + ((back_c >> 4) & 1)
        lane_match = (back_r & (lanes_n - 1)) == from_lane
        back_slot = NZ - 1 - (back_r >> log2(lanes_n))
        for d in range(NX):
            ex[d] = hot(lane_match & (source == (back_slot + d * NZ).astype(F32)))
        token_col[...] = dot(info, hot(iota((128, 128), 0) == token_at))

    def down(d):
        for i in range(len(pieces)):
            if not d:
                send.arrived(h_part(i, chip_lane(d, True)), hpsem.at[i, 0], partner)
            elif d % NY == half:
                for way in range(2):
                    sem = hpsem.at[i, NY if way else d % NY]
                    send.arrived(h_part(i, chip_lane(d, True), half, way), sem, partner)
            else:
                send.arrived(h_part(i, chip_lane(d, True)), hpsem.at[i, d % NY], partner)
        lhs = jnp.concatenate(
            [
                jnp.concatenate(
                    [
                        hg[chip(d) * 2 + c, pl.ds(2 * slot[(e - d) % NY], 2)].reshape(2 * ROWS, 128)
                        for e in range(NY)
                    ],
                    axis=0,
                )
                for c in range(2)
            ],
            axis=1,
        )
        at_col = pl.multiple_of(chip(d) * 256, 256)
        return dot_nt(lhs, w_down[:, pl.ds(at_col, 256)])

    for h in range(2):
        for way in range(2):
            if passes(1, way, h):
                y_hop(way, 1, loc, h)
        p_hop(0, loc, h, h == 0)
    for copy in weight_copies:
        copy.wait()

    def down_step(k):
        for d in sorted({-k % NY, k}):
            acc[...] += down(d)

    acc[...] = jnp.zeros(acc.shape, F32)
    steps = [(float(k), token_step, (k,)) for k in range(1, half + 1)]
    for i, piece in enumerate(pieces):
        far = max(piece)
        steps.append((min(far + 1, half) + (0.5 if far < half else 0.7), gate_up, (i,)))
        for k in range(1, half + 1):
            if strides[i] == 1:
                when = 0.4 + 0.2 * i if k == 1 else k - 1.0 + 0.1 * i
            elif i < len(pieces) - 1:
                when = 1.25 - 0.05 * (k == 2) if k <= 2 else 2.25 + 0.05 * (k == 4)
            else:
                when = 1.65 - 0.05 * (k == 2) if k <= 2 else 3.5 + 0.05 * (k == 4)
            steps.append((half + when, h_step, (i, k)))
    steps.append((half + 1.4, return_map, ()))
    for k in range(half + 1):
        steps.append((half + (3.2 if k < 3 else 4.0), down_step, (k,)))
    for when, step, operands in sorted(steps, key=lambda entry: entry[0]):
        step(*operands)

    result = jnp.where(
        iota((group_rows, 256), 1) == feats, jnp.concatenate([token_col[...]] * 2, axis=1), acc[...]
    ).astype(BF16)
    for q in range(NZ // 4):
        for d in x_order:
            rows = dot(ex[d, pl.ds(q * 4 * lanes_n, 4 * lanes_n)], result).astype(BF16)
            target = rs if d else rr
            target[d, pl.ds(4 * q, 4)] = rows.reshape(4, lanes_n, 256)
            if d:
                send(rs.at[d, pl.ds(4 * q, 4)], rr.at[d, pl.ds(4 * q, 4)], rsem.at[d, q], x_dev(NX - d))

    seen = set()

    def part(j):
        p = NZ - 1 - at[j]
        q = p // 4
        if q not in seen:
            seen.add(q)
            for d in range(1, NX):
                send.arrived(rr.at[d, pl.ds(4 * q, 4)], rsem.at[d, q], x_dev(d))
        sums = [jnp.zeros((lanes_n, 256), F32) for t in range(TOK)]
        for d in range(NX):
            rows = rr[d, p].astype(F32)
            which = jnp.sum(
                jnp.where(iota((lanes_n, 256), 1) == feats, rows, 0.0), axis=1, keepdims=True
            )
            for t in range(TOK):
                sums[t] += jnp.where(which == float(t + 1), rows, 0.0)
        return jnp.concatenate(sums, axis=0)

    def gathered(value, way, k, c):
        piece = value[:, c * 128 : (c + 1) * 128]
        slot = at[way * k % NZ] if k else NZ + (way < 0)
        for step in (1, 2):
            if k + step <= reach[way]:
                send.arrived(rb.at[slot, step - 1, c], bsem.at[slot, step - 1, c], z_dev(way * step))
                piece += rb[slot, step - 1, c].astype(F32)
        return piece

    def z_send(way, k):
        step = 1 if k % 2 else 2
        value = part(way * k % NZ)
        slot = at[way * k % NZ]
        there = at[way * (k - step) % NZ] if k > step else NZ + (way < 0)
        for c in range(2):
            piece = value[:, c * 128 : (c + 1) * 128] if k % 2 else gathered(value, way, k, c)
            sb[slot, c] = piece.astype(BF16)
            send(sb.at[slot, c], rb.at[there, step - 1, c], bsem.at[there, step - 1, c], z_dev(-way * step))

    for k in range(NZ // 2, 0, -2):
        for way, dist in ((1, k), (-1, k), (-1, k - 1), (1, k - 1)):
            if k == NZ // 2 and dist <= reach[way]:
                z_send(way, dist)
        if k > 2:
            for way in (1, -1):
                z_send(way, k - 3)
            for way in (1, -1):
                z_send(way, k - 2)
    value = part(0)
    halves = []
    for c in range(2):
        piece = gathered(value, 1, 0, c) + gathered(jnp.zeros(value.shape, F32), -1, 0, c)
        halves.append(piece.astype(BF16))

    fin_r, fin_c = iota((lanes_n * 8, TOK * lanes_n), 0), iota((lanes_n * 8, TOK * lanes_n), 1)
    fin = ((fin_r >> 3) == (fin_c & (lanes_n - 1))) & ((fin_r & 3) == (fin_c >> log2(lanes_n)))
    upper = ((fin_r >> 2) & 1) == 1
    rows = dot(hot(fin & jnp.logical_not(upper)), halves[0]) + dot(hot(fin & upper), halves[1])
    fs[...] = rows.astype(BF16).reshape(lanes_n, 8, 128)
    for k in range(1, lanes_n):
        lane = lax.rem(loc + k, lanes_n)
        send(fs.at[lane], fr.at[loc], fsem.at[k], (node, lane))
    fr[loc] = fs[loc]
    for k in range(1, lanes_n):
        lane = lax.rem(loc + lanes_n - k, lanes_n)
        send.arrived(fr.at[lane], fsem.at[k], (node, lane))
    whole = []
    for lane in range(lanes_n):
        piece = fr[lane].astype(F32)
        whole += [piece[:TOK]] + ([piece[TOK:, : feats - 128]] if feats > 128 else [])
    out_ref[...] = jnp.concatenate(whole, axis=1).astype(BF16)
    send.drain()


def on_device(tokens, expert_ids, gate_codes, gate_proj, up_proj, down_proj):
    width = tokens.shape[1]
    seg_len = width // SEG
    lanes_n = 2 * NY
    hidden, feats = down_proj.shape
    dma = pltpu.SemaphoreType.DMA
    vmem = pl.BlockSpec(memory_space=pltpu.VMEM)
    hbm = pl.BlockSpec(memory_space=pltpu.HBM)
    half = NY // 2
    return pl.pallas_call(
        kernel,
        out_shape=jax.ShapeDtypeStruct((TOK, width), BF16),
        in_specs=[hbm] * 6,
        out_specs=vmem,
        scratch_shapes=[
            pltpu.VMEM(tokens.shape, BF16),
            pltpu.VMEM(expert_ids.shape, I32),
            pltpu.VMEM(gate_codes.shape, I32),
            pltpu.VMEM((width, 256), BF16),
            pltpu.VMEM((256, hidden), BF16),
            pltpu.VMEM((NZ, PARTS, 16, (seg_len + 128) // PARTS), BF16),
            pltpu.VMEM((NX, NZ // 4, 16, seg_len + 128), BF16),
            pltpu.VMEM((NX, NZ // 4, 16, seg_len + 128), BF16),
            pltpu.VMEM((lanes_n, SEG, ROWS, seg_len), BF16),
            pltpu.VMEM((lanes_n, ROWS, 128), BF16),
            pltpu.VMEM((lanes_n, lanes_n, ROWS, 128), BF16),
            pltpu.VMEM((lanes_n * ROWS, 256), F32),
            pltpu.VMEM((lanes_n * ROWS, 128), F32),
            pltpu.VMEM((NX, NZ * lanes_n, lanes_n * ROWS), BF16),
            pltpu.VMEM((NX, NZ, lanes_n, 256), BF16),
            pltpu.VMEM((NX, NZ, lanes_n, 256), BF16),
            pltpu.VMEM((NZ, 2, TOK * lanes_n, 128), BF16),
            pltpu.VMEM((NZ + 2, 2, 2, TOK * lanes_n, 128), BF16),
            pltpu.VMEM((lanes_n, 8, 128), BF16),
            pltpu.VMEM((lanes_n, 8, 128), BF16),
            dma((6,)),
            dma((SENDS,)),
            dma((NZ, PARTS)),
            dma((NX, NZ // 4)),
            dma((2, half + 1, 2)),
            dma((2, half + 1)),
            dma((NY, 2)),
            dma((NY,)),
            dma((max(half, 2), 2, half + 1)),
            dma((max(half, 2), NY + 1)),
            dma((NX, NZ // 4)),
            dma((NZ + 2, 2, 2)),
            dma((lanes_n,)),
        ],
        compiler_params=pltpu.CompilerParams(
            collective_id=0, has_side_effects=True, vmem_limit_bytes=67_000_000
        ),
        name="moe",
    )(tokens, expert_ids, gate_codes, gate_proj, up_proj, down_proj.T)


def solution(mesh):
    return jax.shard_map(
        on_device,
        mesh=mesh,
        in_specs=(
            P(("node", "local"), None),
            P(("node", "local"), None),
            P(("node", "local"), None),
            P(None, ("node", "local")),
            P(None, ("node", "local")),
            P("node", "local"),
        ),
        out_specs=P(("node", "local"), None),
        check_vma=False,
    )
```
